32 devices in a mesh: members: 2 (over y), lon: 4 (over z), lat: 4 (over x, core).
Axes of the slice: x: 2, y: 2, z: 4, core: 2. Of those that a mesh axis runs over, the one named last changes fastest.
Arguments:
- tokens: bfloat16 [128, 128, 1024], P(('members', 'lat'), 'lon'), parts along dimension 0, may hold values from -24 to 24
- w_query: bfloat16 [1024, 1024], replicated, may hold values from -0.375 to 0.375
- w_key: bfloat16 [1024, 1024], replicated, may hold values from -0.375 to 0.375
- w_value: bfloat16 [1024, 1024], replicated, may hold values from -0.1875 to 0.1875
- w_out: bfloat16 [1024, 1024], replicated, may hold values from -0.1875 to 0.1875
- coarse_gain: float32 [1024], replicated, may hold values from 0.1 to 1.9
Outputs:
- mixed: bfloat16 [128, 128, 1024], P(('members', 'lat'), 'lon'), parts along dimension 0
The draws below stay inside these ranges and needn't reach their ends.
There are 2 independent parts, one for each index of `members`. The reference program is written for one: setup_inputs(seed, part) draws one part's arguments, and reference() takes and returns one part's arrays. A program takes and returns all parts, laid end to end along the dimension named above; an argument that names none is the same for every part. Nothing has to cross between parts.
All inputs are finite; a program needn't handle non-finite values.
Results may differ from the reference program's by a relative error of at most 0.0035.
The reference program's roundings to bfloat16 on the way count: a program that leaves them out, or rounds other values in their place, can miss the bound.
Values may be sent and summed in bfloat16 or wider, within the bound.
A program may use at most 128 MiB of HBM per device.

```python
import jax
import jax.numpy as jnp
from jax import lax

D = 1024
HEADS = 16
HEAD_DIM = 64
RADIUS = 4
POOL = 8
NLAT = 64
NLON = 128


def draw_tokens(key, part):
    first = jax.random.fold_in(key, 0)
    base = jnp.clip(jax.random.normal(first, (NLAT, NLON, D), jnp.float32), -6.0, 6.0)
    return base.astype(jnp.bfloat16)


def bell_draw(own_key, shape, deviation, bound, kind=jnp.bfloat16):
    array = jax.random.normal(own_key, shape, jnp.float32) * deviation
    return jnp.minimum(jnp.maximum(array, -bound), bound).astype(kind)


def setup_inputs(seed: int = 0, part: int = 0) -> dict:
    key_list = jax.random.split(jax.random.key(seed), 7)
    part_keys = jax.random.split(jax.random.fold_in(key_list[6], part), 7)
    tokens = draw_tokens(jax.random.fold_in(jax.random.fold_in(key_list[6], part), 71), part)
    w_query = bell_draw(key_list[1], (D, D), (D // 4) ** -0.5, 0.375)
    w_key = bell_draw(key_list[2], (D, D), (D // 4) ** -0.5, 0.375)
    w_value = bell_draw(key_list[3], (D, D), D ** -0.5, 0.1875)
    w_out = bell_draw(key_list[4], (D, D), D ** -0.5, 0.1875)
    coarse_gain = jnp.clip(1.0 + 0.18 * jax.random.normal(key_list[5], (D,), jnp.float32), 0.1, 1.9)
    return dict(tokens=tokens, w_query=w_query, w_key=w_key, w_value=w_value, w_out=w_out, coarse_gain=coarse_gain)


def reference(tokens, w_query, w_key, w_value, w_out, coarse_gain):
    nlat, nlon, width = tokens.shape
    flat = tokens.reshape(nlat * nlon, width)

    def project(weight):
        return jnp.dot(flat, weight, preferred_element_type=jnp.float32).astype(jnp.bfloat16).reshape(nlat, nlon, width)
    query = project(w_query)
    keys = project(w_key)
    values = project(w_value)
    pooled = tokens.astype(jnp.float32).reshape(nlat // POOL, POOL, nlon // POOL, POOL, width).mean(axis=(1, 3))
    pooled = pooled.reshape(-1, width)
    meansq = lax.optimization_barrier(jnp.mean(pooled * pooled, axis=-1, keepdims=True))
    coarse = (pooled * lax.rsqrt(meansq + 1e-06) * coarse_gain).astype(jnp.bfloat16)
    coarse_keys = jnp.dot(coarse, w_key, preferred_element_type=jnp.float32).astype(jnp.bfloat16)
    coarse_values = jnp.dot(coarse, w_value, preferred_element_type=jnp.float32).astype(jnp.bfloat16)
    far_keys = coarse_keys.astype(jnp.float32).reshape(-1, HEADS, HEAD_DIM)
    far_values = coarse_values.astype(jnp.float32).reshape(-1, HEADS, HEAD_DIM)
    span = 2 * RADIUS + 1
    pad_keys = jnp.pad(keys, ((RADIUS, RADIUS), (0, 0), (0, 0)))
    pad_values = jnp.pad(values, ((RADIUS, RADIUS), (0, 0), (0, 0)))
    scale = HEAD_DIM ** (-0.5)

    def neighbours(padded, row):
        band = lax.dynamic_slice_in_dim(padded, row, span, 0)
        shifted = jnp.stack([jnp.roll(band, -offset, axis=1) for offset in range(-RADIUS, RADIUS + 1)], axis=1)
        return shifted.reshape(span * span, nlon, width).transpose(1, 0, 2).astype(jnp.float32).reshape(nlon, span * span, HEADS, HEAD_DIM)

    def one_row(row):
        qrow = lax.dynamic_index_in_dim(query, row, 0, keepdims=False).astype(jnp.float32).reshape(nlon, HEADS, HEAD_DIM)
        local_keys = neighbours(pad_keys, row)
        local_values = neighbours(pad_values, row)
        rows_of = row + jnp.arange(span, dtype=jnp.int32) - RADIUS
        valid_row = (rows_of >= 0) & (rows_of < nlat)
        valid = jnp.repeat(valid_row, span)
        local = jnp.einsum('jhd,jkhd->hjk', qrow, local_keys) * scale
        local = jnp.where(valid[None, None, :], local, -jnp.inf)
        far = jnp.einsum('jhd,chd->hjc', qrow, far_keys) * scale
        top = jnp.maximum(local.max(axis=-1), far.max(axis=-1))[..., None]
        near_weight = jnp.exp(local - top)
        far_weight = jnp.exp(far - top)
        total = near_weight.sum(axis=-1) + far_weight.sum(axis=-1)
        near_b = lax.optimization_barrier(near_weight.astype(jnp.bfloat16)).astype(jnp.float32)
        far_b = lax.optimization_barrier(far_weight.astype(jnp.bfloat16)).astype(jnp.float32)
        mix = jnp.einsum('hjk,jkhd->jhd', near_b, local_values) + jnp.einsum('hjc,chd->jhd', far_b, far_values)
        return (mix / total.T[:, :, None]).reshape(nlon, width).astype(jnp.bfloat16)
    attended = lax.map(one_row, jnp.arange(nlat, dtype=jnp.int32))
    mixed = jnp.dot(attended.reshape(nlat * nlon, width), w_out, preferred_element_type=jnp.float32)
    return mixed.astype(jnp.bfloat16).reshape(nlat, nlon, width)
```

```python
import functools

import jax
import jax.numpy as jnp
from jax import lax
from jax.experimental import pallas as pl
from jax.experimental.pallas import tpu as pltpu
from jax.sharding import PartitionSpec as P

HEADS = 16
HEAD_DIM = 64
RADIUS = 4
POOL = 8
SIDE = 2 * RADIUS
CW = RADIUS
GROUP = 4
GW = GROUP * HEAD_DIM
MESH = pl.DeviceIdType.MESH
DIRECTIONS = [(da, db) for da in (-1, 0, 1) for db in (-1, 0, 1) if (da, db) != (0, 0)]
SEND_ORDER = sorted(range(len(DIRECTIONS)), key=lambda i: abs(DIRECTIONS[i][0]) + 2 * abs(DIRECTIONS[i][1]) - 3 * (DIRECTIONS[i][1] == 0))
F32 = jnp.float32
BF16 = jnp.bfloat16


def dot(a, b):
    return jnp.dot(a, b, preferred_element_type=F32)


def dot_nt(a, b):
    return lax.dot_general(a, b, (((1,), (1,)), ((), ())), preferred_element_type=F32)


def swap_halves(first, second, low_half):
    lows = jnp.where(low_half, first, pltpu.roll(second, CW, 1))
    highs = jnp.where(low_half, pltpu.roll(first, CW, 1), second)
    return lows, highs


def kernel(
    n_lat, n_lon, tok_hbm, wq_hbm, wk_hbm, wv_hbm, gain_hbm, att,
    tok, gain, x_s, wq, wk, wv, q_s, k_s, v_s, fk_s, fv_s, own, c_s, bias,
    local_sem, halo_send, halo_recv, lon_send, lon_recv, lat_send, lat_recv,
):
    a = lax.axis_index("lat")
    b = lax.axis_index("lon")
    lat_dev, lon_dev, width = tok_hbm.shape
    n_cg = lon_dev // CW
    per_cg = lat_dev * CW
    rows = n_cg * per_cg
    edge = RADIUS * CW
    n_groups = width // GW
    has_up = a > 0
    has_down = a < n_lat - 1

    def guarded(da, fn, receiving):
        step = -da if receiving else da
        if step == 0:
            fn()
        else:
            pl.when(has_up if step < 0 else has_down)(fn)

    loads = [
        pltpu.make_async_copy(src, dst, local_sem.at[i])
        for i, (src, dst) in enumerate(
            [(tok_hbm, tok), (gain_hbm, gain), (wq_hbm, wq), (wk_hbm, wk), (wv_hbm, wv)]
        )
    ]

    lon_of = lambda db: lax.rem(b + db + n_lon, n_lon)

    barrier = pltpu.get_barrier_semaphore()
    for i in range(1, n_lon):
        pl.semaphore_signal(barrier, inc=1, device_id={"lon": lax.rem(b + i, n_lon)}, device_id_type=MESH)
    for i in range(1, n_lat):
        pl.semaphore_signal(barrier, inc=1, device_id={"lat": lax.rem(a + i, n_lat)}, device_id_type=MESH)
    for da in (-1, 1):

        def greet(da=da):
            for db in (-1, 1):
                pl.semaphore_signal(
                    barrier, inc=1, device_id={"lat": a + da, "lon": lon_of(db)}, device_id_type=MESH
                )

        guarded(da, greet, False)
    for load in loads[:2]:
        load.start()

    loads[0].wait()
    for load in loads[2:]:
        load.start()
    loads[1].wait()
    low_half = lax.broadcasted_iota(jnp.int32, (lat_dev // 2, 2 * CW, width), 1) < CW
    for t in range(n_cg // 2):
        pair = tok[:, t * 2 * CW : (t + 1) * 2 * CW, :].astype(F32).reshape(lat_dev // 2, 2, 2 * CW, width)
        even, odd = swap_halves(pair[:, 0], pair[:, 1], low_half)
        x_s[2 * t + 1, edge : edge + per_cg, :] = even.reshape(per_cg, width).astype(BF16)
        x_s[2 * t + 2, edge : edge + per_cg, :] = odd.reshape(per_cg, width).astype(BF16)

    flat = x_s[1 : n_cg + 1, edge : edge + per_cg, :].reshape(rows, width)
    cells_lon = n_cg * CW // POOL
    n_cells = (lat_dev // POOL) * cells_lon
    ti = lax.broadcasted_iota(jnp.int32, (n_cells, rows), 1)
    ci = lax.broadcasted_iota(jnp.int32, (n_cells, rows), 0)
    cell = ((ti % per_cg) // (CW * POOL)) * cells_lon + ti // (per_cg * POOL // CW)
    pick = jnp.where(cell == ci, 1.0 / (POOL * POOL), 0.0).astype(BF16)
    pooled = dot(pick, flat)
    meansq = jnp.mean(pooled * pooled, axis=-1, keepdims=True)
    coarse = (pooled * lax.rsqrt(meansq + 1e-06) * gain[...]).astype(BF16)
    own[...] = coarse
    c_s[a, b] = coarse

    diagonal = 2 * has_up.astype(jnp.int32) + 2 * has_down.astype(jnp.int32)
    pl.semaphore_wait(barrier, n_lon + n_lat - 2 + diagonal)

    def halo(i):
        da, db = DIRECTIONS[i]
        src_rows = {-1: pl.ds(edge, edge), 0: pl.ds(edge, per_cg), 1: pl.ds(per_cg, edge)}[da]
        src_cols = {-1: pl.ds(1, 1), 0: pl.ds(1, n_cg), 1: pl.ds(n_cg, 1)}[db]
        dst_rows = {-1: pl.ds(edge + per_cg, edge), 0: pl.ds(edge, per_cg), 1: pl.ds(0, edge)}[da]
        dst_cols = {-1: pl.ds(n_cg + 1, 1), 0: pl.ds(1, n_cg), 1: pl.ds(0, 1)}[db]
        return pltpu.make_async_remote_copy(
            src_ref=x_s.at[src_cols, src_rows],
            dst_ref=x_s.at[dst_cols, dst_rows],
            send_sem=halo_send.at[i],
            recv_sem=halo_recv.at[i],
            device_id={"lat": a + da, "lon": lon_of(db)},
            device_id_type=MESH,
        )

    def lon_copy(i):
        return pltpu.make_async_remote_copy(
            src_ref=own,
            dst_ref=c_s.at[a, b],
            send_sem=lon_send.at[i],
            recv_sem=lon_recv.at[i],
            device_id={"lon": lax.rem(b + i + 1, n_lon)},
            device_id_type=MESH,
        )

    def lat_copy(i):
        return pltpu.make_async_remote_copy(
            src_ref=c_s.at[a],
            dst_ref=c_s.at[a],
            send_sem=lat_send.at[i],
            recv_sem=lat_recv.at[i],
            device_id={"lat": lax.rem(a + i + 1, n_lat)},
            device_id_type=MESH,
        )

    for i in range(n_lon - 1):
        lon_copy(i).start()
    for i in SEND_ORDER:
        guarded(DIRECTIONS[i][0], lambda i=i: halo(i).start(), False)

    n_rb = lat_dev // SIDE
    nq = SIDE * SIDE
    half = SIDE * CW
    span = 2 * half
    nk = 4 * span
    qi = lax.broadcasted_iota(jnp.int32, (nq, nk), 0)
    ki = lax.broadcasted_iota(jnp.int32, (nq, nk), 1)
    q_row, q_col = (qi % half) // CW, (qi // half) * CW + qi % CW
    k_row, k_col = (ki % span) // CW, (ki // span) * CW + ki % CW
    inside = (k_row >= q_row) & (k_row <= q_row + SIDE) & (k_col >= q_col) & (k_col <= q_col + SIDE)
    for r in range(n_rb):
        g_row = a * lat_dev + r * SIDE + k_row - RADIUS
        ok = inside & (g_row >= 0) & (g_row < n_lat * lat_dev)
        bias[r] = jnp.where(ok, 0.0, -jnp.inf).astype(F32)

    @pl.when(jnp.logical_not(has_up))
    def _():
        x_s[:, 0:edge, :] = jnp.zeros((n_cg + 2, edge, width), BF16)

    @pl.when(jnp.logical_not(has_down))
    def _():
        x_s[:, edge + per_cg : 2 * edge + per_cg, :] = jnp.zeros((n_cg + 2, edge, width), BF16)

    def columns(n):
        return pl.ds(pl.multiple_of(n * GW, GW), GW)

    loads[2].wait()

    @pl.loop(0, n_groups, unroll=4)
    def _(n):
        xv = x_s[1 : n_cg + 1, edge : edge + per_cg, :].reshape(rows, width)
        q = dot(xv, wq[:, columns(n)]) * (HEAD_DIM ** -0.5)
        q_s[n] = q.astype(BF16).reshape(n_cg, per_cg, GW)

    for i in range(n_lon - 1):
        lon_copy(i).wait_recv()
    for i in range(n_lat - 1):
        lat_copy(i).start()

    loads[3].wait()
    loads[4].wait()

    @pl.loop(0, n_groups, unroll=4)
    def _(n):
        xv = x_s[1 : n_cg + 1, edge : edge + per_cg, :].reshape(rows, width)
        for w, dst in ((wk, k_s), (wv, v_s)):
            y = dot(xv, w[:, columns(n)]).astype(BF16)
            dst[n, 1 : n_cg + 1, edge : edge + per_cg, :] = y.reshape(n_cg, per_cg, GW)

    for i in range(n_lat - 1):
        peer = lax.rem(a + n_lat - i - 1, n_lat)
        pltpu.make_async_remote_copy(
            src_ref=c_s.at[a],
            dst_ref=c_s.at[peer],
            send_sem=lat_send.at[i],
            recv_sem=lat_recv.at[i],
            device_id={"lat": lax.rem(a + i + 1, n_lat)},
            device_id_type=MESH,
        ).wait_recv()

    n_far = n_lat * n_lon * n_cells

    @pl.loop(0, n_groups, unroll=4)
    def _(n):
        cv = c_s[...].astype(F32).reshape(n_far, width).astype(BF16)
        for w, dst in ((wk, fk_s), (wv, fv_s)):
            dst[n] = dot(cv, w[:, columns(n)]).astype(BF16)

    low = edge + per_cg
    band = n_cg * edge

    for i, (da, db) in enumerate(DIRECTIONS):
        if db == 0:
            guarded(da, lambda i=i: halo(i).wait_recv(), True)

    @pl.loop(0, n_groups, unroll=4)
    def _(n):
        xv = jnp.concatenate(
            [
                x_s[1 : n_cg + 1, 0:edge, :].reshape(band, width),
                x_s[1 : n_cg + 1, low : low + edge, :].reshape(band, width),
            ],
            axis=0,
        )
        for w, dst in ((wk, k_s), (wv, v_s)):
            y = dot(xv, w[:, columns(n)]).astype(BF16)
            dst[n, 1 : n_cg + 1, 0:edge, :] = y[0:band].reshape(n_cg, edge, GW)
            dst[n, 1 : n_cg + 1, low : low + edge, :] = y[band:].reshape(n_cg, edge, GW)

    n_cb = n_cg // 2
    lane_head = lax.broadcasted_iota(jnp.int32, (nq, GW), 1) // HEAD_DIM
    picks = [jnp.where(lane_head == j, 1.0, 0.0).astype(F32) for j in range(GROUP)]
    picks_b = [p.astype(BF16) for p in picks]

    def attend(n, c):
        fk = fk_s[n]
        fv = fv_s[n]
        for r in range(n_rb):
            q = q_s[n, pl.ds(2 * c, 2), r * half : (r + 1) * half, :].reshape(nq, GW)
            k = k_s[n, pl.ds(2 * c, 4), r * half : r * half + span, :].reshape(nk, GW)
            v = v_s[n, pl.ds(2 * c, 4), r * half : r * half + span, :].reshape(nk, GW)
            q4 = jnp.concatenate([q * p for p in picks_b], axis=0)
            near = dot_nt(q4, k).reshape(GROUP, nq, nk) + bias[r][None]
            score = jnp.concatenate([near.reshape(GROUP * nq, nk), dot_nt(q4, fk)], axis=1)
            weight = jnp.exp(score - jnp.max(score, axis=-1, keepdims=True))
            total = jnp.sum(weight, axis=-1, keepdims=True)
            mix = dot(weight.astype(BF16), jnp.concatenate([v, fv], axis=0))
            mix = mix * (1.0 / total)
            res = mix[0:nq] * picks[0]
            for j in range(1, GROUP):
                res = res + mix[j * nq : (j + 1) * nq] * picks[j]
            att[pl.ds(2 * c, 2), r * half : (r + 1) * half, columns(n)] = res.astype(BF16).reshape(
                2, half, GW
            )

    @pl.loop(0, n_groups * (n_cb - 2), unroll=4)
    def _(step):
        attend(step // (n_cb - 2), 1 + step % (n_cb - 2))

    for i, (da, db) in enumerate(DIRECTIONS):
        if db != 0:
            guarded(da, lambda i=i: halo(i).wait_recv(), True)

    @pl.loop(0, n_groups, unroll=4)
    def _(n):
        xv = jnp.concatenate([x_s[0], x_s[n_cg + 1]], axis=0)
        for w, dst in ((wk, k_s), (wv, v_s)):
            y = dot(xv, w[:, columns(n)]).astype(BF16)
            dst[n, 0] = y[0 : low + edge]
            dst[n, n_cg + 1] = y[low + edge :]

    @pl.loop(0, n_groups * 2, unroll=4)
    def _(step):
        attend(step // 2, (step % 2) * (n_cb - 1))

    for i, (da, db) in enumerate(DIRECTIONS):
        guarded(da, lambda i=i: halo(i).wait_send(), False)
    for i in range(n_lon - 1):
        lon_copy(i).wait_send()
    for i in range(n_lat - 1):
        lat_copy(i).wait_send()


def project(att, wo, out_hbm, out, sem):
    n_cg, per_cg, width = att.shape
    lat_dev, lon_dev, _ = out.shape
    low_half = lax.broadcasted_iota(jnp.int32, (lat_dev // 2, 2 * CW, GW), 1) < CW
    copies = []
    for n in range(width // GW):
        cols = pl.ds(n * GW, GW)
        y = dot(att[...].reshape(n_cg * per_cg, width), wo[:, cols])
        y = y.reshape(n_cg, lat_dev // 2, 2 * CW, GW)
        for t in range(n_cg // 2):
            first, second = swap_halves(y[2 * t], y[2 * t + 1], low_half)
            both = jnp.concatenate([first[:, None], second[:, None]], axis=1)
            out[:, t * 2 * CW : (t + 1) * 2 * CW, cols] = both.reshape(lat_dev, 2 * CW, GW).astype(BF16)
        copies.append(pltpu.make_async_copy(out.at[:, :, cols], out_hbm.at[:, :, cols], sem.at[n]))
        copies[-1].start()
    for copy in copies:
        copy.wait()


def body(tokens, w_query, w_key, w_value, w_out, coarse_gain):
    lat_dev, lon_dev, width = tokens.shape
    n_lat, n_lon = lax.axis_size("lat"), lax.axis_size("lon")
    n_cg = lon_dev // CW
    per_cg = lat_dev * CW
    edge = RADIUS * CW
    n_groups = width // GW
    n_cells = (lat_dev // POOL) * (lon_dev // POOL)
    n_far = n_lat * n_lon * n_cells
    ext = (n_cg + 2, per_cg + 2 * edge)
    vmem = pl.BlockSpec(memory_space=pltpu.VMEM)
    anyspace = pl.BlockSpec(memory_space=pltpu.HBM)
    weight = pltpu.VMEM((width, width), BF16)
    dma = pltpu.SemaphoreType.DMA
    in_hbm = functools.partial(pltpu.with_memory_space_constraint, memory_space=pltpu.HBM)
    att = pl.pallas_call(
        functools.partial(kernel, n_lat, n_lon),
        out_shape=jax.ShapeDtypeStruct((n_cg, per_cg, width), BF16),
        in_specs=[anyspace] * 5,
        out_specs=vmem,
        scratch_shapes=[
            pltpu.VMEM((lat_dev, lon_dev, width), BF16),
            pltpu.VMEM((1, width), F32),
            pltpu.VMEM((*ext, width), BF16),
            weight, weight, weight,
            pltpu.VMEM((n_groups, n_cg, per_cg, GW), BF16),
            pltpu.VMEM((n_groups, *ext, GW), BF16),
            pltpu.VMEM((n_groups, *ext, GW), BF16),
            pltpu.VMEM((n_groups, n_far, GW), BF16),
            pltpu.VMEM((n_groups, n_far, GW), BF16),
            pltpu.VMEM((n_cells, width), BF16),
            pltpu.VMEM((n_lat, n_lon, n_cells, width), BF16),
            pltpu.VMEM((lat_dev // SIDE, SIDE * SIDE, 4 * SIDE * SIDE), F32),
            dma((5,)),
            dma((len(DIRECTIONS),)),
            dma((len(DIRECTIONS),)),
            dma((n_lon - 1,)),
            dma((n_lon - 1,)),
            dma((n_lat - 1,)),
            dma((n_lat - 1,)),
        ],
        compiler_params=pltpu.CompilerParams(
            collective_id=0, has_side_effects=True, vmem_limit_bytes=40 * 1024 * 1024
        ),
    )(*map(in_hbm, (tokens, w_query, w_key, w_value, coarse_gain.reshape(1, width))))
    return pl.pallas_call(
        project,
        out_shape=jax.ShapeDtypeStruct((lat_dev, lon_dev, width), BF16),
        in_specs=[vmem, vmem],
        out_specs=anyspace,
        scratch_shapes=[pltpu.VMEM((lat_dev, lon_dev, width), BF16), dma((n_groups,))],
        compiler_params=pltpu.CompilerParams(vmem_limit_bytes=16 * 1024 * 1024),
    )(att, w_out)


def solution(mesh):
    placed = (P(("members", "lat"), "lon", None), P(), P(), P(), P(), P())
    return jax.shard_map(
        body,
        mesh=mesh,
        in_specs=placed,
        out_specs=P(("members", "lat"), "lon", None),
        check_vma=False,
    )
```

```python
import functools

import jax
import jax.numpy as jnp
from jax import lax
from jax.experimental import pallas as pl
from jax.experimental.pallas import tpu as pltpu
from jax.sharding import PartitionSpec as P

HEADS = 16
HEAD_DIM = 64
RADIUS = 4
POOL = 8
SIDE = 2 * RADIUS
CW = RADIUS
GROUP = 4
GW = GROUP * HEAD_DIM
MESH = pl.DeviceIdType.MESH
DIRECTIONS = [(da, db) for da in (-1, 0, 1) for db in (-1, 0, 1) if (da, db) != (0, 0)]
SEND_ORDER = sorted(range(len(DIRECTIONS)), key=lambda i: abs(DIRECTIONS[i][0]) + 2 * abs(DIRECTIONS[i][1]) - 3 * (DIRECTIONS[i][1] == 0))
F32 = jnp.float32
BF16 = jnp.bfloat16


def dot(a, b):
    return jnp.dot(a, b, preferred_element_type=F32)


def dot_nt(a, b):
    return lax.dot_general(a, b, (((1,), (1,)), ((), ())), preferred_element_type=F32)


def swap_halves(first, second, low_half):
    lows = jnp.where(low_half, first, pltpu.roll(second, CW, 1))
    highs = jnp.where(low_half, pltpu.roll(first, CW, 1), second)
    return lows, highs


def kernel(
    n_lat, n_lon, tok_hbm, wq_hbm, wk_hbm, wv_hbm, gain_hbm, att,
    tok, gain, x_s, wq, wk, wv, q_s, k_s, v_s, fk_s, fv_s, own, c_s, bias,
    local_sem, halo_send, halo_recv, lon_send, lon_recv, lat_send, lat_recv,
):
    a = lax.axis_index("lat")
    b = lax.axis_index("lon")
    lat_dev, lon_dev, width = tok_hbm.shape
    n_cg = lon_dev // CW
    per_cg = lat_dev * CW
    rows = n_cg * per_cg
    edge = RADIUS * CW
    n_groups = width // GW
    has_up = a > 0
    has_down = a < n_lat - 1

    def guarded(da, fn, receiving):
        step = -da if receiving else da
        if step == 0:
            fn()
        else:
            pl.when(has_up if step < 0 else has_down)(fn)

    loads = [
        pltpu.make_async_copy(src, dst, local_sem.at[i])
        for i, (src, dst) in enumerate(
            [(tok_hbm, tok), (gain_hbm, gain), (wq_hbm, wq), (wk_hbm, wk), (wv_hbm, wv)]
        )
    ]

    lon_of = lambda db: lax.rem(b + db + n_lon, n_lon)

    barrier = pltpu.get_barrier_semaphore()
    for i in range(1, n_lon):
        pl.semaphore_signal(barrier, inc=1, device_id={"lon": lax.rem(b + i, n_lon)}, device_id_type=MESH)
    for i in range(1, n_lat):
        pl.semaphore_signal(barrier, inc=1, device_id={"lat": lax.rem(a + i, n_lat)}, device_id_type=MESH)
    for da in (-1, 1):

        def greet(da=da):
            for db in (-1, 1):
                pl.semaphore_signal(
                    barrier, inc=1, device_id={"lat": a + da, "lon": lon_of(db)}, device_id_type=MESH
                )

        guarded(da, greet, False)
    for load in loads[:2]:
        load.start()

    loads[0].wait()
    for load in loads[2:]:
        load.start()
    loads[1].wait()
    flat = tok[...].reshape(rows, width)
    cells_lon = n_cg * CW // POOL
    n_cells = (lat_dev // POOL) * cells_lon
    ti = lax.broadcasted_iota(jnp.int32, (n_cells, rows), 1)
    ci = lax.broadcasted_iota(jnp.int32, (n_cells, rows), 0)
    cell = (ti // (lon_dev * POOL)) * cells_lon + (ti % lon_dev) // POOL
    pick = jnp.where(cell == ci, 1.0 / (POOL * POOL), 0.0).astype(BF16)
    pooled = dot(pick, flat)
    meansq = jnp.mean(pooled * pooled, axis=-1, keepdims=True)
    coarse = (pooled * lax.rsqrt(meansq + 1e-06) * gain[...]).astype(BF16)
    own[...] = coarse
    c_s[a, b] = coarse

    diagonal = 2 * has_up.astype(jnp.int32) + 2 * has_down.astype(jnp.int32)
    pl.semaphore_wait(barrier, n_lon + n_lat - 2 + diagonal)

    def halo(i):
        da, db = DIRECTIONS[i]
        src_rows = {-1: pl.ds(edge, edge), 0: pl.ds(edge, per_cg), 1: pl.ds(per_cg, edge)}[da]
        src_cols = {-1: pl.ds(1, 1), 0: pl.ds(1, n_cg), 1: pl.ds(n_cg, 1)}[db]
        dst_rows = {-1: pl.ds(edge + per_cg, edge), 0: pl.ds(edge, per_cg), 1: pl.ds(0, edge)}[da]
        dst_cols = {-1: pl.ds(n_cg + 1, 1), 0: pl.ds(1, n_cg), 1: pl.ds(0, 1)}[db]
        return pltpu.make_async_remote_copy(
            src_ref=x_s.at[src_cols, src_rows],
            dst_ref=x_s.at[dst_cols, dst_rows],
            send_sem=halo_send.at[i],
            recv_sem=halo_recv.at[i],
            device_id={"lat": a + da, "lon": lon_of(db)},
            device_id_type=MESH,
        )

    def lon_copy(i):
        return pltpu.make_async_remote_copy(
            src_ref=own,
            dst_ref=c_s.at[a, b],
            send_sem=lon_send.at[i],
            recv_sem=lon_recv.at[i],
            device_id={"lon": lax.rem(b + i + 1, n_lon)},
            device_id_type=MESH,
        )

    def lat_copy(i, j, owner=a):
        source = lax.rem(b + n_lon - j, n_lon)
        return pltpu.make_async_remote_copy(
            src_ref=c_s.at[a, source],
            dst_ref=c_s.at[owner, source],
            send_sem=lat_send.at[i, j],
            recv_sem=lat_recv.at[i, j],
            device_id={"lat": lax.rem(a + i + 1, n_lat)},
            device_id_type=MESH,
        )

    for i in range(n_lon - 1):
        lon_copy(i).start()
    for i in range(n_lat - 1):
        lat_copy(i, 0).start()

    low_half = lax.broadcasted_iota(jnp.int32, (lat_dev // 2, 2 * CW, width), 1) < CW
    for t in range(n_cg // 2):
        pair = tok[:, t * 2 * CW : (t + 1) * 2 * CW, :].astype(F32).reshape(lat_dev // 2, 2, 2 * CW, width)
        even, odd = swap_halves(pair[:, 0], pair[:, 1], low_half)
        x_s[2 * t + 1, edge : edge + per_cg, :] = even.reshape(per_cg, width).astype(BF16)
        x_s[2 * t + 2, edge : edge + per_cg, :] = odd.reshape(per_cg, width).astype(BF16)

    for i in SEND_ORDER:
        guarded(DIRECTIONS[i][0], lambda i=i: halo(i).start(), False)

    n_rb = lat_dev // SIDE
    nq = SIDE * SIDE
    half = SIDE * CW
    span = 2 * half
    nk = 4 * span
    qi = lax.broadcasted_iota(jnp.int32, (nq, nk), 0)
    ki = lax.broadcasted_iota(jnp.int32, (nq, nk), 1)
    q_row, q_col = (qi % half) // CW, (qi // half) * CW + qi % CW
    k_row, k_col = (ki % span) // CW, (ki // span) * CW + ki % CW
    inside = (k_row >= q_row) & (k_row <= q_row + SIDE) & (k_col >= q_col) & (k_col <= q_col + SIDE)
    for r in range(n_rb):
        g_row = a * lat_dev + r * SIDE + k_row - RADIUS
        ok = inside & (g_row >= 0) & (g_row < n_lat * lat_dev)
        bias[r] = jnp.where(ok, 0.0, -jnp.inf).astype(F32)

    @pl.when(jnp.logical_not(has_up))
    def _():
        x_s[:, 0:edge, :] = jnp.zeros((n_cg + 2, edge, width), BF16)

    @pl.when(jnp.logical_not(has_down))
    def _():
        x_s[:, edge + per_cg : 2 * edge + per_cg, :] = jnp.zeros((n_cg + 2, edge, width), BF16)

    def columns(n):
        return pl.ds(pl.multiple_of(n * GW, GW), GW)

    loads[2].wait()

    @pl.loop(0, n_groups, unroll=4)
    def _(n):
        xv = x_s[1 : n_cg + 1, edge : edge + per_cg, :].reshape(rows, width)
        q = dot(xv, wq[:, columns(n)]) * (HEAD_DIM ** -0.5)
        q_s[n] = q.astype(BF16).reshape(n_cg, per_cg, GW)

    for j in range(1, n_lon):
        lon_copy(j - 1).wait_recv()
        for i in range(n_lat - 1):
            lat_copy(i, j).start()

    loads[3].wait()
    loads[4].wait()

    @pl.loop(0, n_groups, unroll=4)
    def _(n):
        xv = x_s[1 : n_cg + 1, edge : edge + per_cg, :].reshape(rows, width)
        for w, dst in ((wk, k_s), (wv, v_s)):
            y = dot(xv, w[:, columns(n)]).astype(BF16)
            dst[n, 1 : n_cg + 1, edge : edge + per_cg, :] = y.reshape(n_cg, per_cg, GW)

    low = edge + per_cg
    band = n_cg * edge

    for i, (da, db) in enumerate(DIRECTIONS):
        if db == 0:
            guarded(da, lambda i=i: halo(i).wait_recv(), True)

    @pl.loop(0, n_groups, unroll=4)
    def _(n):
        xv = jnp.concatenate(
            [
                x_s[1 : n_cg + 1, 0:edge, :].reshape(band, width),
                x_s[1 : n_cg + 1, low : low + edge, :].reshape(band, width),
            ],
            axis=0,
        )
        for w, dst in ((wk, k_s), (wv, v_s)):
            y = dot(xv, w[:, columns(n)]).astype(BF16)
            dst[n, 1 : n_cg + 1, 0:edge, :] = y[0:band].reshape(n_cg, edge, GW)
            dst[n, 1 : n_cg + 1, low : low + edge, :] = y[band:].reshape(n_cg, edge, GW)

    for i in range(n_lat - 1):
        for j in range(n_lon):
            lat_copy(i, j, lax.rem(a + n_lat - i - 1, n_lat)).wait_recv()

    n_far = n_lat * n_lon * n_cells

    @pl.loop(0, n_groups, unroll=4)
    def _(n):
        cv = c_s[...].astype(F32).reshape(n_far, width).astype(BF16)
        for w, dst in ((wk, fk_s), (wv, fv_s)):
            dst[n] = dot(cv, w[:, columns(n)]).astype(BF16)

    n_cb = n_cg // 2
    lane_head = lax.broadcasted_iota(jnp.int32, (nq, GW), 1) // HEAD_DIM
    picks = [jnp.where(lane_head == j, 1.0, 0.0).astype(F32) for j in range(GROUP)]
    picks_b = [p.astype(BF16) for p in picks]

    def attend(n, c):
        fk = fk_s[n]
        fv = fv_s[n]
        for r in range(n_rb):
            q = q_s[n, pl.ds(2 * c, 2), r * half : (r + 1) * half, :].reshape(nq, GW)
            k = k_s[n, pl.ds(2 * c, 4), r * half : r * half + span, :].reshape(nk, GW)
            v = v_s[n, pl.ds(2 * c, 4), r * half : r * half + span, :].reshape(nk, GW)
            q4 = jnp.concatenate([q * p for p in picks_b], axis=0)
            near = dot_nt(q4, k).reshape(GROUP, nq, nk) + bias[r][None]
            score = jnp.concatenate([near.reshape(GROUP * nq, nk), dot_nt(q4, fk)], axis=1)
            weight = jnp.exp(score - jnp.max(score, axis=-1, keepdims=True))
            total = jnp.sum(weight, axis=-1, keepdims=True)
            mix = dot(weight.astype(BF16), jnp.concatenate([v, fv], axis=0))
            mix = mix * (1.0 / total)
            res = mix[0:nq] * picks[0]
            for j in range(1, GROUP):
                res = res + mix[j * nq : (j + 1) * nq] * picks[j]
            att[pl.ds(2 * c, 2), r * half : (r + 1) * half, columns(n)] = res.astype(BF16).reshape(
                2, half, GW
            )

    @pl.loop(0, n_groups * (n_cb - 2), unroll=8)
    def _(step):
        attend(step // (n_cb - 2), 1 + step % (n_cb - 2))

    for i, (da, db) in enumerate(DIRECTIONS):
        if db != 0:
            guarded(da, lambda i=i: halo(i).wait_recv(), True)

    @pl.loop(0, n_groups, unroll=4)
    def _(n):
        xv = jnp.concatenate([x_s[0], x_s[n_cg + 1]], axis=0)
        for w, dst in ((wk, k_s), (wv, v_s)):
            y = dot(xv, w[:, columns(n)]).astype(BF16)
            dst[n, 0] = y[0 : low + edge]
            dst[n, n_cg + 1] = y[low + edge :]

    @pl.loop(0, n_groups * 2, unroll=8)
    def _(step):
        attend(step // 2, (step % 2) * (n_cb - 1))

    for i, (da, db) in enumerate(DIRECTIONS):
        guarded(da, lambda i=i: halo(i).wait_send(), False)
    for i in range(n_lon - 1):
        lon_copy(i).wait_send()
    for i in range(n_lat - 1):
        for j in range(n_lon):
            lat_copy(i, j).wait_send()


def project(att, wo, out_hbm, out, sem):
    n_cg, per_cg, width = att.shape
    lat_dev, lon_dev, _ = out.shape
    low_half = lax.broadcasted_iota(jnp.int32, (lat_dev // 2, 2 * CW, GW), 1) < CW
    copies = []
    for n in range(width // GW):
        cols = pl.ds(n * GW, GW)
        y = dot(att[...].reshape(n_cg * per_cg, width), wo[:, cols])
        y = y.reshape(n_cg, lat_dev // 2, 2 * CW, GW)
        for t in range(n_cg // 2):
            first, second = swap_halves(y[2 * t], y[2 * t + 1], low_half)
            both = jnp.concatenate([first[:, None], second[:, None]], axis=1)
            out[:, t * 2 * CW : (t + 1) * 2 * CW, cols] = both.reshape(lat_dev, 2 * CW, GW).astype(BF16)
        copies.append(pltpu.make_async_copy(out.at[:, :, cols], out_hbm.at[:, :, cols], sem.at[n]))
        copies[-1].start()
    for copy in copies:
        copy.wait()


def body(tokens, w_query, w_key, w_value, w_out, coarse_gain):
    lat_dev, lon_dev, width = tokens.shape
    n_lat, n_lon = lax.axis_size("lat"), lax.axis_size("lon")
    n_cg = lon_dev // CW
    per_cg = lat_dev * CW
    edge = RADIUS * CW
    n_groups = width // GW
    n_cells = (lat_dev // POOL) * (lon_dev // POOL)
    n_far = n_lat * n_lon * n_cells
    ext = (n_cg + 2, per_cg + 2 * edge)
    vmem = pl.BlockSpec(memory_space=pltpu.VMEM)
    anyspace = pl.BlockSpec(memory_space=pltpu.HBM)
    weight = pltpu.VMEM((width, width), BF16)
    dma = pltpu.SemaphoreType.DMA
    in_hbm = functools.partial(pltpu.with_memory_space_constraint, memory_space=pltpu.HBM)
    att = pl.pallas_call(
        functools.partial(kernel, n_lat, n_lon),
        out_shape=jax.ShapeDtypeStruct((n_cg, per_cg, width), BF16),
        in_specs=[anyspace] * 5,
        out_specs=vmem,
        scratch_shapes=[
            pltpu.VMEM((lat_dev, lon_dev, width), BF16),
            pltpu.VMEM((1, width), F32),
            pltpu.VMEM((*ext, width), BF16),
            weight, weight, weight,
            pltpu.VMEM((n_groups, n_cg, per_cg, GW), BF16),
            pltpu.VMEM((n_groups, *ext, GW), BF16),
            pltpu.VMEM((n_groups, *ext, GW), BF16),
            pltpu.VMEM((n_groups, n_far, GW), BF16),
            pltpu.VMEM((n_groups, n_far, GW), BF16),
            pltpu.VMEM((n_cells, width), BF16),
            pltpu.VMEM((n_lat, n_lon, n_cells, width), BF16),
            pltpu.VMEM((lat_dev // SIDE, SIDE * SIDE, 4 * SIDE * SIDE), F32),
            dma((5,)),
            dma((len(DIRECTIONS),)),
            dma((len(DIRECTIONS),)),
            dma((n_lon - 1,)),
            dma((n_lon - 1,)),
            dma((n_lat - 1, n_lon)),
            dma((n_lat - 1, n_lon)),
        ],
        compiler_params=pltpu.CompilerParams(
            collective_id=0, has_side_effects=True, vmem_limit_bytes=40 * 1024 * 1024
        ),
    )(*map(in_hbm, (tokens, w_query, w_key, w_value, coarse_gain.reshape(1, width))))
    return pl.pallas_call(
        project,
        out_shape=jax.ShapeDtypeStruct((lat_dev, lon_dev, width), BF16),
        in_specs=[vmem, vmem],
        out_specs=anyspace,
        scratch_shapes=[pltpu.VMEM((lat_dev, lon_dev, width), BF16), dma((n_groups,))],
        compiler_params=pltpu.CompilerParams(vmem_limit_bytes=16 * 1024 * 1024),
    )(att, w_out)


def solution(mesh):
    placed = (P(("members", "lat"), "lon", None), P(), P(), P(), P(), P())
    return jax.shard_map(
        body,
        mesh=mesh,
        in_specs=placed,
        out_specs=P(("members", "lat"), "lon", None),
        check_vma=False,
    )
```

```python
import functools

import jax
import jax.numpy as jnp
from jax import lax
from jax.experimental import pallas as pl
from jax.experimental.pallas import tpu as pltpu
from jax.sharding import PartitionSpec as P

HEADS = 16
HEAD_DIM = 64
RADIUS = 4
POOL = 8
SIDE = 2 * RADIUS
CW = RADIUS
GROUP = 4
TOKEN_PARTS = 4
GW = GROUP * HEAD_DIM
MESH = pl.DeviceIdType.MESH
DIRECTIONS = [(da, db) for da in (-1, 0, 1) for db in (-1, 0, 1) if (da, db) != (0, 0)]
SEND_ORDER = sorted(range(len(DIRECTIONS)), key=lambda i: abs(DIRECTIONS[i][0]) + 2 * abs(DIRECTIONS[i][1]) - 3 * (DIRECTIONS[i][1] == 0))
F32 = jnp.float32
BF16 = jnp.bfloat16


def dot(a, b):
    return jnp.dot(a, b, preferred_element_type=F32)


def dot_nt(a, b):
    return lax.dot_general(a, b, (((1,), (1,)), ((), ())), preferred_element_type=F32)


def swap_halves(first, second, low_half):
    lows = jnp.where(low_half, first, pltpu.roll(second, CW, 1))
    highs = jnp.where(low_half, pltpu.roll(first, CW, 1), second)
    return lows, highs


def kernel(
    n_lat, n_lon, tok_hbm, wq_hbm, wk_hbm, wv_hbm, gain_hbm, att,
    tok, gain, x_s, wq, wk, wv, q_s, k_s, v_s, fk_s, fv_s, own, c_s, bias,
    piece_sem, local_sem, halo_send, halo_recv, lon_send, lon_recv, lat_send, lat_recv,
):
    a = lax.axis_index("lat")
    b = lax.axis_index("lon")
    lat_dev, lon_dev, width = tok_hbm.shape
    n_cg = lon_dev // CW
    per_cg = lat_dev * CW
    rows = n_cg * per_cg
    edge = RADIUS * CW
    n_groups = width // GW
    has_up = a > 0
    has_down = a < n_lat - 1

    def guarded(da, fn, receiving):
        step = -da if receiving else da
        if step == 0:
            fn()
        else:
            pl.when(has_up if step < 0 else has_down)(fn)

    loads = [
        pltpu.make_async_copy(src, dst, local_sem.at[i])
        for i, (src, dst) in enumerate(
            [(gain_hbm, gain), (wq_hbm, wq), (wk_hbm, wk), (wv_hbm, wv)]
        )
    ]

    lon_of = lambda db: lax.rem(b + db + n_lon, n_lon)

    barrier = pltpu.get_barrier_semaphore()
    for i in range(1, n_lon):
        pl.semaphore_signal(barrier, inc=1, device_id={"lon": lax.rem(b + i, n_lon)}, device_id_type=MESH)
    for i in range(1, n_lat):
        pl.semaphore_signal(barrier, inc=1, device_id={"lat": lax.rem(a + i, n_lat)}, device_id_type=MESH)
    for da in (-1, 1):

        def greet(da=da):
            for db in (-1, 1):
                pl.semaphore_signal(
                    barrier, inc=1, device_id={"lat": a + da, "lon": lon_of(db)}, device_id_type=MESH
                )

        guarded(da, greet, False)
    part = lat_dev // TOKEN_PARTS
    pieces = [
        pltpu.make_async_copy(tok_hbm.at[pl.ds(i * part, part)], tok.at[pl.ds(i * part, part)], piece_sem.at[i])
        for i in range(TOKEN_PARTS)
    ]
    for load in [*pieces, loads[0]]:
        load.start()

    cells_lon = n_cg * CW // POOL
    n_cells = (lat_dev // POOL) * cells_lon
    ti = lax.broadcasted_iota(jnp.int32, (n_cells, rows), 1)
    ci = lax.broadcasted_iota(jnp.int32, (n_cells, rows), 0)
    cell = (ti // (lon_dev * POOL)) * cells_lon + (ti % lon_dev) // POOL
    pick = jnp.where(cell == ci, 1.0 / (POOL * POOL), 0.0).astype(BF16)
    n_rb = lat_dev // SIDE
    nq = SIDE * SIDE
    half = SIDE * CW
    span = 2 * half
    nk = 4 * span
    qi = lax.broadcasted_iota(jnp.int32, (nq, nk), 0)
    ki = lax.broadcasted_iota(jnp.int32, (nq, nk), 1)
    q_row, q_col = (qi % half) // CW, (qi // half) * CW + qi % CW
    k_row, k_col = (ki % span) // CW, (ki // span) * CW + ki % CW
    inside = (k_row >= q_row) & (k_row <= q_row + SIDE) & (k_col >= q_col) & (k_col <= q_col + SIDE)
    for r in range(n_rb):
        g_row = a * lat_dev + r * SIDE + k_row - RADIUS
        ok = inside & (g_row >= 0) & (g_row < n_lat * lat_dev)
        bias[r] = jnp.where(ok, 0.0, -jnp.inf).astype(F32)

    @pl.when(jnp.logical_not(has_up))
    def _():
        x_s[:, 0:edge, :] = jnp.zeros((n_cg + 2, edge, width), BF16)

    @pl.when(jnp.logical_not(has_down))
    def _():
        x_s[:, edge + per_cg : 2 * edge + per_cg, :] = jnp.zeros((n_cg + 2, edge, width), BF16)

    for piece in pieces:
        piece.wait()
    for load in loads[1:]:
        load.start()
    loads[0].wait()
    flat = tok[...].reshape(rows, width)
    pooled = dot(pick, flat)
    meansq = jnp.mean(pooled * pooled, axis=-1, keepdims=True)
    coarse = (pooled * lax.rsqrt(meansq + 1e-06) * gain[...]).astype(BF16)
    own[...] = coarse
    c_s[a, b] = coarse

    diagonal = 2 * has_up.astype(jnp.int32) + 2 * has_down.astype(jnp.int32)
    pl.semaphore_wait(barrier, n_lon + n_lat - 2 + diagonal)

    def halo(i):
        da, db = DIRECTIONS[i]
        src_rows = {-1: pl.ds(edge, edge), 0: pl.ds(edge, per_cg), 1: pl.ds(per_cg, edge)}[da]
        src_cols = {-1: pl.ds(1, 1), 0: pl.ds(1, n_cg), 1: pl.ds(n_cg, 1)}[db]
        dst_rows = {-1: pl.ds(edge + per_cg, edge), 0: pl.ds(edge, per_cg), 1: pl.ds(0, edge)}[da]
        dst_cols = {-1: pl.ds(n_cg + 1, 1), 0: pl.ds(1, n_cg), 1: pl.ds(0, 1)}[db]
        return pltpu.make_async_remote_copy(
            src_ref=x_s.at[src_cols, src_rows],
            dst_ref=x_s.at[dst_cols, dst_rows],
            send_sem=halo_send.at[i],
            recv_sem=halo_recv.at[i],
            device_id={"lat": a + da, "lon": lon_of(db)},
            device_id_type=MESH,
        )

    def lon_copy(i):
        return pltpu.make_async_remote_copy(
            src_ref=own,
            dst_ref=c_s.at[a, b],
            send_sem=lon_send.at[i],
            recv_sem=lon_recv.at[i],
            device_id={"lon": lax.rem(b + i + 1, n_lon)},
            device_id_type=MESH,
        )

    def lat_copy(i, j, owner=a):
        source = lax.rem(b + n_lon - j, n_lon)
        return pltpu.make_async_remote_copy(
            src_ref=c_s.at[a, source],
            dst_ref=c_s.at[owner, source],
            send_sem=lat_send.at[i, j],
            recv_sem=lat_recv.at[i, j],
            device_id={"lat": lax.rem(a + i + 1, n_lat)},
            device_id_type=MESH,
        )

    for i in range(n_lon - 1):
        lon_copy(i).start()
    for i in range(n_lat - 1):
        lat_copy(i, 0).start()

    low_half = lax.broadcasted_iota(jnp.int32, (lat_dev // 2, 2 * CW, width), 1) < CW
    for t in range(n_cg // 2):
        pair = tok[:, t * 2 * CW : (t + 1) * 2 * CW, :].astype(F32).reshape(lat_dev // 2, 2, 2 * CW, width)
        even, odd = swap_halves(pair[:, 0], pair[:, 1], low_half)
        x_s[2 * t + 1, edge : edge + per_cg, :] = even.reshape(per_cg, width).astype(BF16)
        x_s[2 * t + 2, edge : edge + per_cg, :] = odd.reshape(per_cg, width).astype(BF16)

    for i in [j for j in SEND_ORDER if DIRECTIONS[j][1] == 0]:
        guarded(DIRECTIONS[i][0], lambda i=i: halo(i).start(), False)

    lower = b < n_lon // 2
    left, right = DIRECTIONS.index((0, -1)), DIRECTIONS.index((0, 1))

    @pl.when(lower)
    def _():
        halo(left).start()

    @pl.when(jnp.logical_not(lower))
    def _():
        halo(right).start()

    def columns(n):
        return pl.ds(pl.multiple_of(n * GW, GW), GW)

    loads[1].wait()

    @pl.loop(0, n_groups, unroll=4)
    def _(n):
        xv = x_s[1 : n_cg + 1, edge : edge + per_cg, :].reshape(rows, width)
        q = dot(xv, wq[:, columns(n)]) * (HEAD_DIM ** -0.5)
        q_s[n] = q.astype(BF16).reshape(n_cg, per_cg, GW)

    for j in range(1, n_lon):
        lon_copy(j - 1).wait_recv()
        for i in range(n_lat - 1):
            lat_copy(i, j).start()

    for i in [j for j in SEND_ORDER if 0 not in DIRECTIONS[j]]:
        guarded(DIRECTIONS[i][0], lambda i=i: halo(i).start(), False)

    @pl.when(lower)
    def _():
        halo(right).start()

    @pl.when(jnp.logical_not(lower))
    def _():
        halo(left).start()

    loads[2].wait()
    loads[3].wait()

    @pl.loop(0, n_groups, unroll=4)
    def _(n):
        xv = x_s[1 : n_cg + 1, edge : edge + per_cg, :].reshape(rows, width)
        for w, dst in ((wk, k_s), (wv, v_s)):
            y = dot(xv, w[:, columns(n)]).astype(BF16)
            dst[n, 1 : n_cg + 1, edge : edge + per_cg, :] = y.reshape(n_cg, per_cg, GW)

    low = edge + per_cg
    band = n_cg * edge

    for i, (da, db) in enumerate(DIRECTIONS):
        if db == 0:
            guarded(da, lambda i=i: halo(i).wait_recv(), True)

    @pl.loop(0, n_groups, unroll=4)
    def _(n):
        xv = jnp.concatenate(
            [
                x_s[1 : n_cg + 1, 0:edge, :].reshape(band, width),
                x_s[1 : n_cg + 1, low : low + edge, :].reshape(band, width),
            ],
            axis=0,
        )
        for w, dst in ((wk, k_s), (wv, v_s)):
            y = dot(xv, w[:, columns(n)]).astype(BF16)
            dst[n, 1 : n_cg + 1, 0:edge, :] = y[0:band].reshape(n_cg, edge, GW)
            dst[n, 1 : n_cg + 1, low : low + edge, :] = y[band:].reshape(n_cg, edge, GW)

    for i in range(n_lat - 1):
        for j in range(n_lon):
            lat_copy(i, j, lax.rem(a + n_lat - i - 1, n_lat)).wait_recv()

    n_far = n_lat * n_lon * n_cells

    @pl.loop(0, n_groups, unroll=4)
    def _(n):
        cv = c_s[...].astype(F32).reshape(n_far, width).astype(BF16)
        for w, dst in ((wk, fk_s), (wv, fv_s)):
            dst[n] = dot(cv, w[:, columns(n)]).astype(BF16)

    n_cb = n_cg // 2
    lane_head = lax.broadcasted_iota(jnp.int32, (nq, GW), 1) // HEAD_DIM
    picks_b = [jnp.where(lane_head == j, 1.0, 0.0).astype(BF16) for j in range(GROUP)]
    lanes = 2 * HEAD_DIM
    left_head = lax.broadcasted_iota(jnp.int32, (nq, lanes), 1) < HEAD_DIM

    def attend(n, c):
        fk = fk_s[n]
        fv = fv_s[n]
        for r in range(n_rb):
            q = q_s[n, pl.ds(2 * c, 2), r * half : (r + 1) * half, :].reshape(nq, GW)
            k = k_s[n, pl.ds(2 * c, 4), r * half : r * half + span, :].reshape(nk, GW)
            v = v_s[n, pl.ds(2 * c, 4), r * half : r * half + span, :].reshape(nk, GW)
            q4 = jnp.concatenate([q * p for p in picks_b], axis=0)
            near = dot_nt(q4, k).reshape(GROUP, nq, nk) + bias[r][None]
            score = jnp.concatenate([near.reshape(GROUP * nq, nk), dot_nt(q4, fk)], axis=1)
            weight = jnp.exp(score - jnp.max(score, axis=-1, keepdims=True))
            total = jnp.sum(weight, axis=-1, keepdims=True)
            mix = dot(weight.astype(BF16), jnp.concatenate([v, fv], axis=0))
            scale = 1.0 / total
            for pair in range(GROUP // 2):
                both = [
                    mix[j * nq : (j + 1) * nq, pair * lanes : (pair + 1) * lanes] * scale[j * nq : (j + 1) * nq]
                    for j in (2 * pair, 2 * pair + 1)
                ]
                att[
                    pl.ds(2 * c, 2),
                    r * half : (r + 1) * half,
                    pl.ds(pl.multiple_of(n * GW + pair * lanes, lanes), lanes),
                ] = jnp.where(left_head, *both).astype(BF16).reshape(2, half, lanes)

    @pl.loop(0, n_groups * (n_cb - 2), unroll=8)
    def _(step):
        attend(step // (n_cb - 2), 1 + step % (n_cb - 2))

    for i, (da, db) in enumerate(DIRECTIONS):
        if db != 0:
            guarded(da, lambda i=i: halo(i).wait_recv(), True)

    @pl.loop(0, n_groups, unroll=4)
    def _(n):
        xv = jnp.concatenate([x_s[0], x_s[n_cg + 1]], axis=0)
        for w, dst in ((wk, k_s), (wv, v_s)):
            y = dot(xv, w[:, columns(n)]).astype(BF16)
            dst[n, 0] = y[0 : low + edge]
            dst[n, n_cg + 1] = y[low + edge :]

    @pl.loop(0, n_groups * 2, unroll=8)
    def _(step):
        attend(step // 2, (step % 2) * (n_cb - 1))

    for i, (da, db) in enumerate(DIRECTIONS):
        guarded(da, lambda i=i: halo(i).wait_send(), False)
    for i in range(n_lon - 1):
        lon_copy(i).wait_send()
    for i in range(n_lat - 1):
        for j in range(n_lon):
            lat_copy(i, j).wait_send()


def project(att, wo, out_hbm, out, sem):
    n_cg, per_cg, width = att.shape
    lat_dev, lon_dev, _ = out.shape
    low_half = lax.broadcasted_iota(jnp.int32, (lat_dev // 2, 2 * CW, GW), 1) < CW
    copies = []
    for n in range(width // GW):
        cols = pl.ds(n * GW, GW)
        y = dot(att[...].reshape(n_cg * per_cg, width), wo[:, cols])
        y = y.reshape(n_cg, lat_dev // 2, 2 * CW, GW)
        for t in range(n_cg // 2):
            first, second = swap_halves(y[2 * t], y[2 * t + 1], low_half)
            both = jnp.concatenate([first[:, None], second[:, None]], axis=1)
            out[:, t * 2 * CW : (t + 1) * 2 * CW, cols] = both.reshape(lat_dev, 2 * CW, GW).astype(BF16)
        copies.append(pltpu.make_async_copy(out.at[:, :, cols], out_hbm.at[:, :, cols], sem.at[n]))
        copies[-1].start()
    for copy in copies:
        copy.wait()


def body(tokens, w_query, w_key, w_value, w_out, coarse_gain):
    lat_dev, lon_dev, width = tokens.shape
    n_lat, n_lon = lax.axis_size("lat"), lax.axis_size("lon")
    n_cg = lon_dev // CW
    per_cg = lat_dev * CW
    edge = RADIUS * CW
    n_groups = width // GW
    n_cells = (lat_dev // POOL) * (lon_dev // POOL)
    n_far = n_lat * n_lon * n_cells
    ext = (n_cg + 2, per_cg + 2 * edge)
    vmem = pl.BlockSpec(memory_space=pltpu.VMEM)
    anyspace = pl.BlockSpec(memory_space=pltpu.HBM)
    weight = pltpu.VMEM((width, width), BF16)
    dma = pltpu.SemaphoreType.DMA
    in_hbm = functools.partial(pltpu.with_memory_space_constraint, memory_space=pltpu.HBM)
    att = pl.pallas_call(
        functools.partial(kernel, n_lat, n_lon),
        out_shape=jax.ShapeDtypeStruct((n_cg, per_cg, width), BF16),
        in_specs=[anyspace] * 5,
        out_specs=vmem,
        scratch_shapes=[
            pltpu.VMEM((lat_dev, lon_dev, width), BF16),
            pltpu.VMEM((1, width), F32),
            pltpu.VMEM((*ext, width), BF16),
            weight, weight, weight,
            pltpu.VMEM((n_groups, n_cg, per_cg, GW), BF16),
            pltpu.VMEM((n_groups, *ext, GW), BF16),
            pltpu.VMEM((n_groups, *ext, GW), BF16),
            pltpu.VMEM((n_groups, n_far, GW), BF16),
            pltpu.VMEM((n_groups, n_far, GW), BF16),
            pltpu.VMEM((n_cells, width), BF16),
            pltpu.VMEM((n_lat, n_lon, n_cells, width), BF16),
            pltpu.VMEM((lat_dev // SIDE, SIDE * SIDE, 4 * SIDE * SIDE), F32),
            dma((TOKEN_PARTS,)),
            dma((4,)),
            dma((len(DIRECTIONS),)),
            dma((len(DIRECTIONS),)),
            dma((n_lon - 1,)),
            dma((n_lon - 1,)),
            dma((n_lat - 1, n_lon)),
            dma((n_lat - 1, n_lon)),
        ],
        compiler_params=pltpu.CompilerParams(
            collective_id=0, has_side_effects=True, vmem_limit_bytes=40 * 1024 * 1024
        ),
    )(*map(in_hbm, (tokens, w_query, w_key, w_value, coarse_gain.reshape(1, width))))
    return pl.pallas_call(
        project,
        out_shape=jax.ShapeDtypeStruct((lat_dev, lon_dev, width), BF16),
        in_specs=[vmem, vmem],
        out_specs=anyspace,
        scratch_shapes=[pltpu.VMEM((lat_dev, lon_dev, width), BF16), dma((n_groups,))],
        compiler_params=pltpu.CompilerParams(vmem_limit_bytes=16 * 1024 * 1024),
    )(att, w_out)


def solution(mesh):
    placed = (P(("members", "lat"), "lon", None), P(), P(), P(), P(), P())
    return jax.shard_map(
        body,
        mesh=mesh,
        in_specs=placed,
        out_specs=P(("members", "lat"), "lon", None),
        check_vma=False,
    )
```

```python
import functools

import jax
import jax.numpy as jnp
from jax import lax
from jax.experimental import pallas as pl
from jax.experimental.pallas import tpu as pltpu
from jax.sharding import PartitionSpec as P

HEADS = 16
HEAD_DIM = 64
RADIUS = 4
POOL = 8
SIDE = 2 * RADIUS
CW = RADIUS
GROUP = 4
TOKEN_PARTS = 4
GW = GROUP * HEAD_DIM
MESH = pl.DeviceIdType.MESH
DIRECTIONS = [(da, db) for da in (-1, 0, 1) for db in (-1, 0, 1) if (da, db) != (0, 0)]
SEND_ORDER = sorted(range(len(DIRECTIONS)), key=lambda i: abs(DIRECTIONS[i][0]) + 2 * abs(DIRECTIONS[i][1]) - 3 * (DIRECTIONS[i][1] == 0))
F32 = jnp.float32
BF16 = jnp.bfloat16


def dot(a, b):
    return jnp.dot(a, b, preferred_element_type=F32)


def dot_nt(a, b):
    return lax.dot_general(a, b, (((1,), (1,)), ((), ())), preferred_element_type=F32)


def swap_halves(first, second, low_half):
    lows = jnp.where(low_half, first, pltpu.roll(second, CW, 1))
    highs = jnp.where(low_half, pltpu.roll(first, CW, 1), second)
    return lows, highs


def kernel(
    n_lat, n_lon, tok_hbm, wq_hbm, wk_hbm, wv_hbm, gain_hbm, att,
    tok, gain, x_s, wq, wk, wv, q_s, k_s, v_s, fk_s, fv_s, own, c_s, bias,
    piece_sem, local_sem, halo_send, halo_recv, lon_send, lon_recv, lat_send, lat_recv,
):
    a = lax.axis_index("lat")
    b = lax.axis_index("lon")
    lat_dev, lon_dev, width = tok_hbm.shape
    n_cg = lon_dev // CW
    per_cg = lat_dev * CW
    rows = n_cg * per_cg
    edge = RADIUS * CW
    n_groups = width // GW
    has_up = a > 0
    has_down = a < n_lat - 1

    def guarded(da, fn, receiving):
        step = -da if receiving else da
        if step == 0:
            fn()
        else:
            pl.when(has_up if step < 0 else has_down)(fn)

    loads = [
        pltpu.make_async_copy(src, dst, local_sem.at[i])
        for i, (src, dst) in enumerate(
            [(gain_hbm, gain), (wq_hbm, wq), (wk_hbm, wk), (wv_hbm, wv)]
        )
    ]

    lon_of = lambda db: lax.rem(b + db + n_lon, n_lon)

    barrier = pltpu.get_barrier_semaphore()
    for i in range(1, n_lon):
        pl.semaphore_signal(barrier, inc=1, device_id={"lon": lax.rem(b + i, n_lon)}, device_id_type=MESH)
    for i in range(1, n_lat):
        pl.semaphore_signal(barrier, inc=1, device_id={"lat": lax.rem(a + i, n_lat)}, device_id_type=MESH)
    for da in (-1, 1):

        def greet(da=da):
            for db in (-1, 1):
                pl.semaphore_signal(
                    barrier, inc=1, device_id={"lat": a + da, "lon": lon_of(db)}, device_id_type=MESH
                )

        guarded(da, greet, False)
    part = lat_dev // TOKEN_PARTS
    pieces = [
        pltpu.make_async_copy(tok_hbm.at[pl.ds(i * part, part)], tok.at[pl.ds(i * part, part)], piece_sem.at[i])
        for i in range(TOKEN_PARTS)
    ]
    for load in [*pieces, loads[0]]:
        load.start()

    cells_lon = n_cg * CW // POOL
    n_cells = (lat_dev // POOL) * cells_lon
    ti = lax.broadcasted_iota(jnp.int32, (n_cells, rows), 1)
    ci = lax.broadcasted_iota(jnp.int32, (n_cells, rows), 0)
    cell = (ti // (lon_dev * POOL)) * cells_lon + (ti % lon_dev) // POOL
    pick = jnp.where(cell == ci, 1.0 / (POOL * POOL), 0.0).astype(BF16)
    n_rb = lat_dev // SIDE
    nq = SIDE * SIDE
    half = SIDE * CW
    span = 2 * half
    nk = 4 * span
    qi = lax.broadcasted_iota(jnp.int32, (nq, nk), 0)
    ki = lax.broadcasted_iota(jnp.int32, (nq, nk), 1)
    q_row, q_col = (qi % half) // CW, (qi // half) * CW + qi % CW
    k_row, k_col = (ki % span) // CW, (ki // span) * CW + ki % CW
    inside = (k_row >= q_row) & (k_row <= q_row + SIDE) & (k_col >= q_col) & (k_col <= q_col + SIDE)
    for r in range(n_rb):
        g_row = a * lat_dev + r * SIDE + k_row - RADIUS
        ok = inside & (g_row >= 0) & (g_row < n_lat * lat_dev)
        bias[r] = jnp.where(ok, 0.0, -jnp.inf).astype(F32)

    @pl.when(jnp.logical_not(has_up))
    def _():
        x_s[:, 0:edge, :] = jnp.zeros((n_cg + 2, edge, width), BF16)

    @pl.when(jnp.logical_not(has_down))
    def _():
        x_s[:, edge + per_cg : 2 * edge + per_cg, :] = jnp.zeros((n_cg + 2, edge, width), BF16)

    for piece in pieces:
        piece.wait()
    for load in loads[1:]:
        load.start()
    loads[0].wait()
    flat = tok[...].reshape(rows, width)
    pooled = dot(pick, flat)
    meansq = jnp.mean(pooled * pooled, axis=-1, keepdims=True)
    coarse = (pooled * lax.rsqrt(meansq + 1e-06) * gain[...]).astype(BF16)
    own[...] = coarse
    c_s[a, b] = coarse

    low_half = lax.broadcasted_iota(jnp.int32, (lat_dev // 2, 2 * CW, width), 1) < CW
    for t in range(n_cg // 2):
        pair = tok[:, t * 2 * CW : (t + 1) * 2 * CW, :].astype(F32).reshape(lat_dev // 2, 2, 2 * CW, width)
        even, odd = swap_halves(pair[:, 0], pair[:, 1], low_half)
        x_s[2 * t + 1, edge : edge + per_cg, :] = even.reshape(per_cg, width).astype(BF16)
        x_s[2 * t + 2, edge : edge + per_cg, :] = odd.reshape(per_cg, width).astype(BF16)

    diagonal = 2 * has_up.astype(jnp.int32) + 2 * has_down.astype(jnp.int32)
    pl.semaphore_wait(barrier, n_lon + n_lat - 2 + diagonal)

    def halo(i):
        da, db = DIRECTIONS[i]
        src_rows = {-1: pl.ds(edge, edge), 0: pl.ds(edge, per_cg), 1: pl.ds(per_cg, edge)}[da]
        src_cols = {-1: pl.ds(1, 1), 0: pl.ds(1, n_cg), 1: pl.ds(n_cg, 1)}[db]
        dst_rows = {-1: pl.ds(edge + per_cg, edge), 0: pl.ds(edge, per_cg), 1: pl.ds(0, edge)}[da]
        dst_cols = {-1: pl.ds(n_cg + 1, 1), 0: pl.ds(1, n_cg), 1: pl.ds(0, 1)}[db]
        return pltpu.make_async_remote_copy(
            src_ref=x_s.at[src_cols, src_rows],
            dst_ref=x_s.at[dst_cols, dst_rows],
            send_sem=halo_send.at[i],
            recv_sem=halo_recv.at[i],
            device_id={"lat": a + da, "lon": lon_of(db)},
            device_id_type=MESH,
        )

    def lon_copy(i):
        return pltpu.make_async_remote_copy(
            src_ref=own,
            dst_ref=c_s.at[a, b],
            send_sem=lon_send.at[i],
            recv_sem=lon_recv.at[i],
            device_id={"lon": lax.rem(b + i + 1, n_lon)},
            device_id_type=MESH,
        )

    def lat_copy(i, j, owner=a):
        source = lax.rem(b + n_lon - j, n_lon)
        return pltpu.make_async_remote_copy(
            src_ref=c_s.at[a, source],
            dst_ref=c_s.at[owner, source],
            send_sem=lat_send.at[i, j],
            recv_sem=lat_recv.at[i, j],
            device_id={"lat": lax.rem(a + i + 1, n_lat)},
            device_id_type=MESH,
        )

    for i in [j for j in SEND_ORDER if DIRECTIONS[j][1] == 0]:
        guarded(DIRECTIONS[i][0], lambda i=i: halo(i).start(), False)

    for i in range(n_lon - 1):
        lon_copy(i).start()
    for i in range(n_lat - 1):
        lat_copy(i, 0).start()

    lower = b < n_lon // 2
    left, right = DIRECTIONS.index((0, -1)), DIRECTIONS.index((0, 1))

    @pl.when(lower)
    def _():
        halo(left).start()

    @pl.when(jnp.logical_not(lower))
    def _():
        halo(right).start()

    def columns(n):
        return pl.ds(pl.multiple_of(n * GW, GW), GW)

    loads[1].wait()

    @pl.loop(0, n_groups, unroll=4)
    def _(n):
        xv = x_s[1 : n_cg + 1, edge : edge + per_cg, :].reshape(rows, width)
        q = dot(xv, wq[:, columns(n)]) * (HEAD_DIM ** -0.5)
        q_s[n] = q.astype(BF16).reshape(n_cg, per_cg, GW)

    for j in range(1, n_lon):
        lon_copy(j - 1).wait_recv()
        for i in range(n_lat - 1):
            lat_copy(i, j).start()

    for i in [j for j in SEND_ORDER if 0 not in DIRECTIONS[j]]:
        guarded(DIRECTIONS[i][0], lambda i=i: halo(i).start(), False)

    @pl.when(lower)
    def _():
        halo(right).start()

    @pl.when(jnp.logical_not(lower))
    def _():
        halo(left).start()

    loads[2].wait()
    loads[3].wait()

    @pl.loop(0, n_groups, unroll=4)
    def _(n):
        xv = x_s[1 : n_cg + 1, edge : edge + per_cg, :].reshape(rows, width)
        for w, dst in ((wk, k_s), (wv, v_s)):
            y = dot(xv, w[:, columns(n)]).astype(BF16)
            dst[n, 1 : n_cg + 1, edge : edge + per_cg, :] = y.reshape(n_cg, per_cg, GW)

    low = edge + per_cg
    band = n_cg * edge

    for i, (da, db) in enumerate(DIRECTIONS):
        if db == 0:
            guarded(da, lambda i=i: halo(i).wait_recv(), True)

    @pl.loop(0, n_groups, unroll=4)
    def _(n):
        xv = jnp.concatenate(
            [
                x_s[1 : n_cg + 1, 0:edge, :].reshape(band, width),
                x_s[1 : n_cg + 1, low : low + edge, :].reshape(band, width),
            ],
            axis=0,
        )
        for w, dst in ((wk, k_s), (wv, v_s)):
            y = dot(xv, w[:, columns(n)]).astype(BF16)
            dst[n, 1 : n_cg + 1, 0:edge, :] = y[0:band].reshape(n_cg, edge, GW)
            dst[n, 1 : n_cg + 1, low : low + edge, :] = y[band:].reshape(n_cg, edge, GW)

    for i in range(n_lat - 1):
        for j in range(n_lon):
            lat_copy(i, j, lax.rem(a + n_lat - i - 1, n_lat)).wait_recv()

    n_far = n_lat * n_lon * n_cells

    @pl.loop(0, n_groups, unroll=4)
    def _(n):
        cv = c_s[...].astype(F32).reshape(n_far, width).astype(BF16)
        for w, dst in ((wk, fk_s), (wv, fv_s)):
            dst[n] = dot(cv, w[:, columns(n)]).astype(BF16)

    n_cb = n_cg // 2
    lane_head = lax.broadcasted_iota(jnp.int32, (nq, GW), 1) // HEAD_DIM
    picks_b = [jnp.where(lane_head == j, 1.0, 0.0).astype(BF16) for j in range(GROUP)]
    lanes = 2 * HEAD_DIM
    left_head = lax.broadcasted_iota(jnp.int32, (nq, lanes), 1) < HEAD_DIM

    def attend(n, c):
        fk = fk_s[n]
        fv = fv_s[n]
        for r in range(n_rb):
            q = q_s[n, pl.ds(2 * c, 2), r * half : (r + 1) * half, :].reshape(nq, GW)
            k = k_s[n, pl.ds(2 * c, 4), r * half : r * half + span, :].reshape(nk, GW)
            v = v_s[n, pl.ds(2 * c, 4), r * half : r * half + span, :].reshape(nk, GW)
            q4 = jnp.concatenate([q * p for p in picks_b], axis=0)
            near = dot_nt(q4, k).reshape(GROUP, nq, nk) + bias[r][None]
            score = jnp.concatenate([near.reshape(GROUP * nq, nk), dot_nt(q4, fk)], axis=1)
            weight = jnp.exp(score - jnp.max(score, axis=-1, keepdims=True))
            total = jnp.sum(weight, axis=-1, keepdims=True)
            mix = dot(weight.astype(BF16), jnp.concatenate([v, fv], axis=0))
            scale = 1.0 / total
            for pair in range(GROUP // 2):
                rows_of = [slice(j * nq, (j + 1) * nq) for j in (2 * pair, 2 * pair + 1)]
                both = [mix[at, pair * lanes : (pair + 1) * lanes] for at in rows_of]
                by = jnp.where(left_head, *(scale[at] for at in rows_of))
                att[
                    pl.ds(2 * c, 2),
                    r * half : (r + 1) * half,
                    pl.ds(pl.multiple_of(n * GW + pair * lanes, lanes), lanes),
                ] = (jnp.where(left_head, *both) * by).astype(BF16).reshape(2, half, lanes)

    @pl.loop(0, n_groups * (n_cb - 2), unroll=8)
    def _(step):
        attend(step // (n_cb - 2), 1 + step % (n_cb - 2))

    for i, (da, db) in enumerate(DIRECTIONS):
        if db != 0:
            guarded(da, lambda i=i: halo(i).wait_recv(), True)

    @pl.loop(0, n_groups, unroll=4)
    def _(n):
        xv = jnp.concatenate([x_s[0], x_s[n_cg + 1]], axis=0)
        for w, dst in ((wk, k_s), (wv, v_s)):
            y = dot(xv, w[:, columns(n)]).astype(BF16)
            dst[n, 0] = y[0 : low + edge]
            dst[n, n_cg + 1] = y[low + edge :]

    @pl.loop(0, n_groups * 2, unroll=8)
    def _(step):
        attend(step // 2, (step % 2) * (n_cb - 1))

    for i, (da, db) in enumerate(DIRECTIONS):
        guarded(da, lambda i=i: halo(i).wait_send(), False)
    for i in range(n_lon - 1):
        lon_copy(i).wait_send()
    for i in range(n_lat - 1):
        for j in range(n_lon):
            lat_copy(i, j).wait_send()


def project(att, wo, out_hbm, out, sem):
    n_cg, per_cg, width = att.shape
    group = 2 * GW
    lat_dev, lon_dev, _ = out.shape
    low_half = lax.broadcasted_iota(jnp.int32, (lat_dev // 2, 2 * CW, group), 1) < CW
    copies = []
    for n in range(width // group):
        cols = pl.ds(n * group, group)
        y = dot(att[...].reshape(n_cg * per_cg, width), wo[:, cols])
        y = y.reshape(n_cg, lat_dev // 2, 2 * CW, group)
        for t in range(n_cg // 2):
            first, second = swap_halves(y[2 * t], y[2 * t + 1], low_half)
            both = jnp.concatenate([first[:, None], second[:, None]], axis=1)
            out[:, t * 2 * CW : (t + 1) * 2 * CW, cols] = both.reshape(lat_dev, 2 * CW, group).astype(BF16)
        copies.append(pltpu.make_async_copy(out.at[:, :, cols], out_hbm.at[:, :, cols], sem.at[n]))
        copies[-1].start()
    for copy in copies:
        copy.wait()


def body(tokens, w_query, w_key, w_value, w_out, coarse_gain):
    lat_dev, lon_dev, width = tokens.shape
    n_lat, n_lon = lax.axis_size("lat"), lax.axis_size("lon")
    n_cg = lon_dev // CW
    per_cg = lat_dev * CW
    edge = RADIUS * CW
    n_groups = width // GW
    n_cells = (lat_dev // POOL) * (lon_dev // POOL)
    n_far = n_lat * n_lon * n_cells
    ext = (n_cg + 2, per_cg + 2 * edge)
    vmem = pl.BlockSpec(memory_space=pltpu.VMEM)
    anyspace = pl.BlockSpec(memory_space=pltpu.HBM)
    weight = pltpu.VMEM((width, width), BF16)
    dma = pltpu.SemaphoreType.DMA
    in_hbm = functools.partial(pltpu.with_memory_space_constraint, memory_space=pltpu.HBM)
    att = pl.pallas_call(
        functools.partial(kernel, n_lat, n_lon),
        out_shape=jax.ShapeDtypeStruct((n_cg, per_cg, width), BF16),
        in_specs=[anyspace] * 5,
        out_specs=vmem,
        scratch_shapes=[
            pltpu.VMEM((lat_dev, lon_dev, width), BF16),
            pltpu.VMEM((1, width), F32),
            pltpu.VMEM((*ext, width), BF16),
            weight, weight, weight,
            pltpu.VMEM((n_groups, n_cg, per_cg, GW), BF16),
            pltpu.VMEM((n_groups, *ext, GW), BF16),
            pltpu.VMEM((n_groups, *ext, GW), BF16),
            pltpu.VMEM((n_groups, n_far, GW), BF16),
            pltpu.VMEM((n_groups, n_far, GW), BF16),
            pltpu.VMEM((n_cells, width), BF16),
            pltpu.VMEM((n_lat, n_lon, n_cells, width), BF16),
            pltpu.VMEM((lat_dev // SIDE, SIDE * SIDE, 4 * SIDE * SIDE), F32),
            dma((TOKEN_PARTS,)),
            dma((4,)),
            dma((len(DIRECTIONS),)),
            dma((len(DIRECTIONS),)),
            dma((n_lon - 1,)),
            dma((n_lon - 1,)),
            dma((n_lat - 1, n_lon)),
            dma((n_lat - 1, n_lon)),
        ],
        compiler_params=pltpu.CompilerParams(
            collective_id=0, has_side_effects=True, vmem_limit_bytes=40 * 1024 * 1024
        ),
    )(*map(in_hbm, (tokens, w_query, w_key, w_value, coarse_gain.reshape(1, width))))
    return pl.pallas_call(
        project,
        out_shape=jax.ShapeDtypeStruct((lat_dev, lon_dev, width), BF16),
        in_specs=[vmem, vmem],
        out_specs=anyspace,
        scratch_shapes=[pltpu.VMEM((lat_dev, lon_dev, width), BF16), dma((n_groups,))],
        compiler_params=pltpu.CompilerParams(vmem_limit_bytes=16 * 1024 * 1024),
    )(att, w_out)


def solution(mesh):
    placed = (P(("members", "lat"), "lon", None), P(), P(), P(), P(), P())
    return jax.shard_map(
        body,
        mesh=mesh,
        in_specs=placed,
        out_specs=P(("members", "lat"), "lon", None),
        check_vma=False,
    )
```

```python
import functools

import jax
import jax.numpy as jnp
from jax import lax
from jax.experimental import pallas as pl
from jax.experimental.pallas import tpu as pltpu
from jax.sharding import PartitionSpec as P

HEADS = 16
HEAD_DIM = 64
RADIUS = 4
POOL = 8
SIDE = 2 * RADIUS
CW = RADIUS
GROUP = 4
TOKEN_PARTS = 4
GW = GROUP * HEAD_DIM
MESH = pl.DeviceIdType.MESH
DIRECTIONS = [(da, db) for da in (-1, 0, 1) for db in (-1, 0, 1) if (da, db) != (0, 0)]
SEND_ORDER = sorted(range(len(DIRECTIONS)), key=lambda i: abs(DIRECTIONS[i][0]) + 2 * abs(DIRECTIONS[i][1]) - 3 * (DIRECTIONS[i][1] == 0))
F32 = jnp.float32
BF16 = jnp.bfloat16


def dot(a, b):
    return jnp.dot(a, b, preferred_element_type=F32)


def dot_nt(a, b):
    return lax.dot_general(a, b, (((1,), (1,)), ((), ())), preferred_element_type=F32)


def swap_halves(first, second, low_half):
    lows = jnp.where(low_half, first, pltpu.roll(second, CW, 1))
    highs = jnp.where(low_half, pltpu.roll(first, CW, 1), second)
    return lows, highs


def kernel(
    n_lat, n_lon, tok_hbm, wq_hbm, wk_hbm, wv_hbm, gain_hbm, att,
    tok, gain, x_s, wq, wk, wv, q_s, k_s, v_s, fk_s, fv_s, own, c_s, bias,
    piece_sem, local_sem, halo_send, halo_recv, lon_send, lon_recv, lat_send, lat_recv,
):
    a = lax.axis_index("lat")
    b = lax.axis_index("lon")
    lat_dev, lon_dev, width = tok_hbm.shape
    n_cg = lon_dev // CW
    per_cg = lat_dev * CW
    rows = n_cg * per_cg
    edge = RADIUS * CW
    n_groups = width // GW
    has_up = a > 0
    has_down = a < n_lat - 1

    def guarded(da, fn, receiving):
        step = -da if receiving else da
        if step == 0:
            fn()
        else:
            pl.when(has_up if step < 0 else has_down)(fn)

    loads = [
        pltpu.make_async_copy(src, dst, local_sem.at[i])
        for i, (src, dst) in enumerate(
            [(gain_hbm, gain), (wq_hbm, wq), (wk_hbm, wk), (wv_hbm, wv)]
        )
    ]

    lon_of = lambda db: lax.rem(b + db + n_lon, n_lon)

    barrier = pltpu.get_barrier_semaphore()
    for i in range(1, n_lon):
        pl.semaphore_signal(barrier, inc=1, device_id={"lon": lax.rem(b + i, n_lon)}, device_id_type=MESH)
    for i in range(1, n_lat):
        pl.semaphore_signal(barrier, inc=1, device_id={"lat": lax.rem(a + i, n_lat)}, device_id_type=MESH)
    for da in (-1, 1):

        def greet(da=da):
            for db in (-1, 1):
                pl.semaphore_signal(
                    barrier, inc=1, device_id={"lat": a + da, "lon": lon_of(db)}, device_id_type=MESH
                )

        guarded(da, greet, False)
    part = lat_dev // TOKEN_PARTS
    pieces = [
        pltpu.make_async_copy(tok_hbm.at[pl.ds(i * part, part)], tok.at[pl.ds(i * part, part)], piece_sem.at[i])
        for i in range(TOKEN_PARTS)
    ]
    for load in [*pieces, loads[0]]:
        load.start()

    cells_lon = n_cg * CW // POOL
    n_cells = (lat_dev // POOL) * cells_lon
    ti = lax.broadcasted_iota(jnp.int32, (n_cells, rows), 1)
    ci = lax.broadcasted_iota(jnp.int32, (n_cells, rows), 0)
    cell = (ti // (lon_dev * POOL)) * cells_lon + (ti % lon_dev) // POOL
    pick = jnp.where(cell == ci, 1.0 / (POOL * POOL), 0.0).astype(BF16)
    n_rb = lat_dev // SIDE
    nq = SIDE * SIDE
    half = SIDE * CW
    span = 2 * half
    nk = 4 * span
    qi = lax.broadcasted_iota(jnp.int32, (nq, nk), 0)
    ki = lax.broadcasted_iota(jnp.int32, (nq, nk), 1)
    q_row, q_col = (qi % half) // CW, (qi // half) * CW + qi % CW
    k_row, k_col = (ki % span) // CW, (ki // span) * CW + ki % CW
    inside = (k_row >= q_row) & (k_row <= q_row + SIDE) & (k_col >= q_col) & (k_col <= q_col + SIDE)
    for r in range(n_rb):
        g_row = a * lat_dev + r * SIDE + k_row - RADIUS
        ok = inside & (g_row >= 0) & (g_row < n_lat * lat_dev)
        bias[r] = jnp.where(ok, 0.0, -jnp.inf).astype(F32)

    @pl.when(jnp.logical_not(has_up))
    def _():
        x_s[:, 0:edge, :] = jnp.zeros((n_cg + 2, edge, width), BF16)

    @pl.when(jnp.logical_not(has_down))
    def _():
        x_s[:, edge + per_cg : 2 * edge + per_cg, :] = jnp.zeros((n_cg + 2, edge, width), BF16)

    for piece in pieces:
        piece.wait()
    for load in loads[1:]:
        load.start()
    loads[0].wait()
    flat = tok[...].reshape(rows, width)
    pooled = dot(pick, flat)
    meansq = jnp.mean(pooled * pooled, axis=-1, keepdims=True)
    coarse = (pooled * lax.rsqrt(meansq + 1e-06) * gain[...]).astype(BF16)
    own[...] = coarse
    c_s[a, b] = coarse

    low_half = lax.broadcasted_iota(jnp.int32, (lat_dev // 2, 2 * CW, width), 1) < CW
    for t in range(n_cg // 2):
        pair = tok[:, t * 2 * CW : (t + 1) * 2 * CW, :].astype(F32).reshape(lat_dev // 2, 2, 2 * CW, width)
        even, odd = swap_halves(pair[:, 0], pair[:, 1], low_half)
        x_s[2 * t + 1, edge : edge + per_cg, :] = even.reshape(per_cg, width).astype(BF16)
        x_s[2 * t + 2, edge : edge + per_cg, :] = odd.reshape(per_cg, width).astype(BF16)

    diagonal = 2 * has_up.astype(jnp.int32) + 2 * has_down.astype(jnp.int32)
    pl.semaphore_wait(barrier, n_lon + n_lat - 2 + diagonal)

    def halo(i):
        da, db = DIRECTIONS[i]
        src_rows = {-1: pl.ds(edge, edge), 0: pl.ds(edge, per_cg), 1: pl.ds(per_cg, edge)}[da]
        src_cols = {-1: pl.ds(1, 1), 0: pl.ds(1, n_cg), 1: pl.ds(n_cg, 1)}[db]
        dst_rows = {-1: pl.ds(edge + per_cg, edge), 0: pl.ds(edge, per_cg), 1: pl.ds(0, edge)}[da]
        dst_cols = {-1: pl.ds(n_cg + 1, 1), 0: pl.ds(1, n_cg), 1: pl.ds(0, 1)}[db]
        return pltpu.make_async_remote_copy(
            src_ref=x_s.at[src_cols, src_rows],
            dst_ref=x_s.at[dst_cols, dst_rows],
            send_sem=halo_send.at[i],
            recv_sem=halo_recv.at[i],
            device_id={"lat": a + da, "lon": lon_of(db)},
            device_id_type=MESH,
        )

    def lon_copy(i):
        return pltpu.make_async_remote_copy(
            src_ref=own,
            dst_ref=c_s.at[a, b],
            send_sem=lon_send.at[i],
            recv_sem=lon_recv.at[i],
            device_id={"lon": lax.rem(b + i + 1, n_lon)},
            device_id_type=MESH,
        )

    def lat_copy(i, j, owner=a):
        source = lax.rem(b + n_lon - j, n_lon)
        return pltpu.make_async_remote_copy(
            src_ref=c_s.at[a, source],
            dst_ref=c_s.at[owner, source],
            send_sem=lat_send.at[i, j],
            recv_sem=lat_recv.at[i, j],
            device_id={"lat": lax.rem(a + i + 1, n_lat)},
            device_id_type=MESH,
        )

    for i in range(n_lon - 1):
        lon_copy(i).start()
    for i in range(n_lat - 1):
        lat_copy(i, 0).start()

    for i in [j for j in SEND_ORDER if DIRECTIONS[j][1] == 0]:
        guarded(DIRECTIONS[i][0], lambda i=i: halo(i).start(), False)

    lower = b < n_lon // 2
    left, right = DIRECTIONS.index((0, -1)), DIRECTIONS.index((0, 1))

    @pl.when(lower)
    def _():
        halo(left).start()

    @pl.when(jnp.logical_not(lower))
    def _():
        halo(right).start()

    def columns(n):
        return pl.ds(pl.multiple_of(n * GW, GW), GW)

    loads[1].wait()

    @pl.loop(0, n_groups, unroll=4)
    def _(n):
        xv = x_s[1 : n_cg + 1, edge : edge + per_cg, :].reshape(rows, width)
        q = dot(xv, wq[:, columns(n)]) * (HEAD_DIM ** -0.5)
        q_s[n] = q.astype(BF16).reshape(n_cg, per_cg, GW)

    for j in range(1, n_lon):
        lon_copy(j - 1).wait_recv()
        for i in range(n_lat - 1):
            lat_copy(i, j).start()

    for i in [j for j in SEND_ORDER if 0 not in DIRECTIONS[j]]:
        guarded(DIRECTIONS[i][0], lambda i=i: halo(i).start(), False)

    @pl.when(lower)
    def _():
        halo(right).start()

    @pl.when(jnp.logical_not(lower))
    def _():
        halo(left).start()

    loads[2].wait()
    loads[3].wait()

    @pl.loop(0, n_groups, unroll=4)
    def _(n):
        xv = x_s[1 : n_cg + 1, edge : edge + per_cg, :].reshape(rows, width)
        for w, dst in ((wk, k_s), (wv, v_s)):
            y = dot(xv, w[:, columns(n)]).astype(BF16)
            dst[n, 1 : n_cg + 1, edge : edge + per_cg, :] = y.reshape(n_cg, per_cg, GW)

    low = edge + per_cg
    band = n_cg * edge

    core = lax.rem(a, 2)
    above = core * low

    def await_band(da):
        i = DIRECTIONS.index((da, 0))
        guarded(da, lambda: halo(i).wait_recv(), True)

    def await_bands(when_odd, when_even):
        pl.when(core == 1)(lambda: await_band(when_odd))
        pl.when(core == 0)(lambda: await_band(when_even))

    def band_kv(start):
        at = pl.ds(pl.multiple_of(start, edge), edge)

        @pl.loop(0, n_groups, unroll=4)
        def _(n):
            xv = x_s[1 : n_cg + 1, at, :].reshape(band, width)
            for w, dst in ((wk, k_s), (wv, v_s)):
                dst[n, 1 : n_cg + 1, at, :] = dot(xv, w[:, columns(n)]).astype(BF16).reshape(n_cg, edge, GW)

    await_bands(1, -1)
    band_kv(low - above)

    await_bands(-1, 1)
    band_kv(above)

    for i in range(n_lat - 1):
        for j in range(n_lon):
            lat_copy(i, j, lax.rem(a + n_lat - i - 1, n_lat)).wait_recv()

    n_far = n_lat * n_lon * n_cells

    @pl.loop(0, n_groups, unroll=4)
    def _(n):
        cv = c_s[...].astype(F32).reshape(n_far, width).astype(BF16)
        for w, dst in ((wk, fk_s), (wv, fv_s)):
            dst[n] = dot(cv, w[:, columns(n)]).astype(BF16)

    n_cb = n_cg // 2
    lane_head = lax.broadcasted_iota(jnp.int32, (nq, GW), 1) // HEAD_DIM
    picks_b = [jnp.where(lane_head == j, 1.0, 0.0).astype(BF16) for j in range(GROUP)]
    lanes = 2 * HEAD_DIM
    left_head = lax.broadcasted_iota(jnp.int32, (nq, lanes), 1) < HEAD_DIM

    def attend(n, c):
        fk = fk_s[n]
        fv = fv_s[n]
        for r in range(n_rb):
            q = q_s[n, pl.ds(2 * c, 2), r * half : (r + 1) * half, :].reshape(nq, GW)
            k = k_s[n, pl.ds(2 * c, 4), r * half : r * half + span, :].reshape(nk, GW)
            v = v_s[n, pl.ds(2 * c, 4), r * half : r * half + span, :].reshape(nk, GW)
            q4 = jnp.concatenate([q * p for p in picks_b], axis=0)
            near = dot_nt(q4, k).reshape(GROUP, nq, nk) + bias[r][None]
            score = jnp.concatenate([near.reshape(GROUP * nq, nk), dot_nt(q4, fk)], axis=1)
            weight = jnp.exp(score - jnp.max(score, axis=-1, keepdims=True))
            total = jnp.sum(weight, axis=-1, keepdims=True)
            mix = dot(weight.astype(BF16), jnp.concatenate([v, fv], axis=0))
            scale = 1.0 / total
            for pair in range(GROUP // 2):
                both = [
                    mix[j * nq : (j + 1) * nq, pair * lanes : (pair + 1) * lanes] * scale[j * nq : (j + 1) * nq]
                    for j in (2 * pair, 2 * pair + 1)
                ]
                att[
                    pl.ds(2 * c, 2),
                    r * half : (r + 1) * half,
                    pl.ds(pl.multiple_of(n * GW + pair * lanes, lanes), lanes),
                ] = jnp.where(left_head, *both).astype(BF16).reshape(2, half, lanes)

    @pl.loop(0, n_groups * (n_cb - 2), unroll=8)
    def _(step):
        attend(step // (n_cb - 2), 1 + step % (n_cb - 2))

    for i, (da, db) in enumerate(DIRECTIONS):
        if db != 0:
            guarded(da, lambda i=i: halo(i).wait_recv(), True)

    @pl.loop(0, n_groups, unroll=4)
    def _(n):
        xv = jnp.concatenate([x_s[0], x_s[n_cg + 1]], axis=0)
        for w, dst in ((wk, k_s), (wv, v_s)):
            y = dot(xv, w[:, columns(n)]).astype(BF16)
            dst[n, 0] = y[0 : low + edge]
            dst[n, n_cg + 1] = y[low + edge :]

    @pl.loop(0, n_groups * 2, unroll=8)
    def _(step):
        attend(step // 2, (step % 2) * (n_cb - 1))

    for i, (da, db) in enumerate(DIRECTIONS):
        guarded(da, lambda i=i: halo(i).wait_send(), False)
    for i in range(n_lon - 1):
        lon_copy(i).wait_send()
    for i in range(n_lat - 1):
        for j in range(n_lon):
            lat_copy(i, j).wait_send()


def project(att, wo, out_hbm, out, sem):
    n_cg, per_cg, width = att.shape
    group = 2 * GW
    lat_dev, lon_dev, _ = out.shape
    low_half = lax.broadcasted_iota(jnp.int32, (lat_dev // 2, 2 * CW, group), 1) < CW
    copies = []
    for n in range(width // group):
        cols = pl.ds(n * group, group)
        y = dot(att[...].reshape(n_cg * per_cg, width), wo[:, cols])
        y = y.reshape(n_cg, lat_dev // 2, 2 * CW, group)
        for t in range(n_cg // 2):
            first, second = swap_halves(y[2 * t], y[2 * t + 1], low_half)
            both = jnp.concatenate([first[:, None], second[:, None]], axis=1)
            out[:, t * 2 * CW : (t + 1) * 2 * CW, cols] = both.reshape(lat_dev, 2 * CW, group).astype(BF16)
        copies.append(pltpu.make_async_copy(out.at[:, :, cols], out_hbm.at[:, :, cols], sem.at[n]))
        copies[-1].start()
    for copy in copies:
        copy.wait()


def body(tokens, w_query, w_key, w_value, w_out, coarse_gain):
    lat_dev, lon_dev, width = tokens.shape
    n_lat, n_lon = lax.axis_size("lat"), lax.axis_size("lon")
    n_cg = lon_dev // CW
    per_cg = lat_dev * CW
    edge = RADIUS * CW
    n_groups = width // GW
    n_cells = (lat_dev // POOL) * (lon_dev // POOL)
    n_far = n_lat * n_lon * n_cells
    ext = (n_cg + 2, per_cg + 2 * edge)
    vmem = pl.BlockSpec(memory_space=pltpu.VMEM)
    anyspace = pl.BlockSpec(memory_space=pltpu.HBM)
    weight = pltpu.VMEM((width, width), BF16)
    dma = pltpu.SemaphoreType.DMA
    in_hbm = functools.partial(pltpu.with_memory_space_constraint, memory_space=pltpu.HBM)
    att = pl.pallas_call(
        functools.partial(kernel, n_lat, n_lon),
        out_shape=jax.ShapeDtypeStruct((n_cg, per_cg, width), BF16),
        in_specs=[anyspace] * 5,
        out_specs=vmem,
        scratch_shapes=[
            pltpu.VMEM((lat_dev, lon_dev, width), BF16),
            pltpu.VMEM((1, width), F32),
            pltpu.VMEM((*ext, width), BF16),
            weight, weight, weight,
            pltpu.VMEM((n_groups, n_cg, per_cg, GW), BF16),
            pltpu.VMEM((n_groups, *ext, GW), BF16),
            pltpu.VMEM((n_groups, *ext, GW), BF16),
            pltpu.VMEM((n_groups, n_far, GW), BF16),
            pltpu.VMEM((n_groups, n_far, GW), BF16),
            pltpu.VMEM((n_cells, width), BF16),
            pltpu.VMEM((n_lat, n_lon, n_cells, width), BF16),
            pltpu.VMEM((lat_dev // SIDE, SIDE * SIDE, 4 * SIDE * SIDE), F32),
            dma((TOKEN_PARTS,)),
            dma((4,)),
            dma((len(DIRECTIONS),)),
            dma((len(DIRECTIONS),)),
            dma((n_lon - 1,)),
            dma((n_lon - 1,)),
            dma((n_lat - 1, n_lon)),
            dma((n_lat - 1, n_lon)),
        ],
        compiler_params=pltpu.CompilerParams(
            collective_id=0, has_side_effects=True, vmem_limit_bytes=40 * 1024 * 1024
        ),
    )(*map(in_hbm, (tokens, w_query, w_key, w_value, coarse_gain.reshape(1, width))))
    return pl.pallas_call(
        project,
        out_shape=jax.ShapeDtypeStruct((lat_dev, lon_dev, width), BF16),
        in_specs=[vmem, vmem],
        out_specs=anyspace,
        scratch_shapes=[pltpu.VMEM((lat_dev, lon_dev, width), BF16), dma((n_groups,))],
        compiler_params=pltpu.CompilerParams(vmem_limit_bytes=16 * 1024 * 1024),
    )(att, w_out)


def solution(mesh):
    placed = (P(("members", "lat"), "lon", None), P(), P(), P(), P(), P())
    return jax.shard_map(
        body,
        mesh=mesh,
        in_specs=placed,
        out_specs=P(("members", "lat"), "lon", None),
        check_vma=False,
    )
```
